128 devices in a mesh: queue: 32 (over y, z, core), batch: 4 (over x).
Axes of the slice: x: 4, y: 4, z: 4, core: 2. Of those that a mesh axis runs over, the one named last changes fastest.
Arguments:
- queries: bfloat16 [16384, 256], P(('queue', 'batch')), may hold values from -160 to 160
- keys: bfloat16 [16384, 256], P(('queue', 'batch')), may hold values from -0.5 to 0.5
- queue_keys: bfloat16 [131072, 256], P('queue'), may hold values from -2 to 2
- log_scale: float32 [1], replicated, may hold values from 0 to 1
- write_pointer: int32 [1], replicated, may hold values from 0 to 1023
- block_order: int32 [128], replicated, may hold values from 0 to 127, each once
- pos_index: int32 [16384], P(('queue', 'batch')), may hold values from 0 to 127
Outputs:
- loss: float32 [16384], P(('queue', 'batch'))
- temp_grad: float32 [1], replicated
- new_queue: bfloat16 [131072, 256], P('queue')
The draws below stay inside these ranges and needn't reach their ends.
Inputs may be any that keep to these rules, and one draw needn't show every extreme that they name: `block_order`: each number of 0 to 127 appears once.
All inputs are finite; a program needn't handle non-finite values.
Results may differ from the reference program's by a relative error of at most 0.0004.
Values may be sent and summed in bfloat16 or wider, within the bound.
A program may use at most 64 MiB of HBM per device.

```python
import jax
import jax.numpy as jnp
from jax import lax

D = 256
BLOCK = 128
TOK_DEV = 128
B = 16384
QUEUE = 131072
NEWBLK = 128
QBLOCKS = 1024


def shared_queue(key):
    base = jax.random.normal(jax.random.fold_in(key, 11), (QUEUE, D), jnp.float32)
    base = jnp.clip(base, -8.0, 8.0) * 0.0625
    return base


def draw_queue_keys(key, part):
    return shared_queue(key).astype(jnp.bfloat16)


def draw_queries(key, part):
    base = jnp.clip(jax.random.normal(jax.random.fold_in(key, 21), (B, D), jnp.float32), -6.0, 6.0)
    return base.astype(jnp.bfloat16)


def touch_ends(drawn, rng, smallest, top_value):
    dims = drawn.shape
    place = [jax.random.randint(jax.random.fold_in(rng, axis), (), 0, dims[axis]) for axis in range(len(dims))]
    drawn = drawn.at[tuple(place)].set(smallest)
    longest = dims.index(max(dims))
    place[longest] = (place[longest] + 1) % dims[longest]
    return drawn.at[tuple(place)].set(top_value)


def block_scale(own_key, dims, split, smallest, high):
    def one(axis_at, parts):
        heights = jax.random.uniform(jax.random.fold_in(jax.random.fold_in(own_key, 6), axis_at), (parts,), jnp.float32, smallest / len(split), high / len(split))
        return jnp.repeat(jnp.exp(heights), dims[axis_at] // parts).reshape((-1,) + (1,) * (len(dims) - axis_at - 1))

    level = one(*split[0])
    for cut in split[1:]:
        level = level * one(*cut)
    return level


def gaussian(own_key, extent, scale, reach, pieces=(), held_as=jnp.bfloat16):
    entries = scale * jax.random.normal(own_key, extent, jnp.float32)
    if pieces:
        entries = entries * block_scale(own_key, extent, pieces, -0.22, 0.18)
    return jnp.clip(entries, -reach, reach).astype(held_as)


def setup_inputs(seed: int = 0) -> dict:
    splits = jax.random.split(jax.random.key(seed), 8)
    queries = draw_queries(jax.random.fold_in(splits[7], 71), 0)
    keys = gaussian(splits[1], (B, D), 0.0625, 0.5, ((0, 128),))
    queue_keys = draw_queue_keys(jax.random.fold_in(splits[7], 71), 0)
    log_scale = jnp.clip(jax.random.uniform(splits[3], (1,), jnp.float32, 0.0, 1.0), 0.0, 1.0)
    write_pointer = jax.random.randint(splits[4], (1,), 0, QBLOCKS).astype(jnp.int32)
    block_order = jax.random.permutation(splits[5], NEWBLK).astype(jnp.int32)
    pos_index = touch_ends(jax.random.randint(splits[6], (B,), 0, TOK_DEV), jax.random.fold_in(splits[6], 1), 0, TOK_DEV - 1).astype(jnp.int32)
    return dict(queries=queries, keys=keys, queue_keys=queue_keys, log_scale=log_scale, write_pointer=write_pointer, block_order=block_order, pos_index=pos_index)


def block_stats(query_block, queue_keys, scale):
    logits = scale * jnp.dot(query_block, queue_keys.T, preferred_element_type=jnp.float32)
    highest = jnp.max(logits, axis=1)
    weights = jnp.exp(logits - highest[:, None])
    return highest, jnp.sum(weights, axis=1), jnp.sum(weights * logits, axis=1)


def reference(queries, keys, queue_keys, log_scale, write_pointer, block_order, pos_index):
    scale = jnp.exp(log_scale[0])
    total_rows = queries.shape[0]
    groups = total_rows // TOK_DEV
    grouped_q = queries.reshape(groups, TOK_DEV, D).astype(jnp.float32)
    grouped_k = keys.reshape(groups, TOK_DEV, D).astype(jnp.float32)
    local_scores = jnp.einsum("gtd,gsd->gts", grouped_q, grouped_k)
    picked = jnp.take_along_axis(local_scores, pos_index.reshape(groups, TOK_DEV, 1).astype(jnp.int32), axis=2)
    pos = scale * picked.reshape(total_rows)
    width = min(512, total_rows)
    blocks = queries.reshape(total_rows // width, width, D)
    peak, total, weighted = lax.map(lambda block_rows: block_stats(block_rows, queue_keys, scale), blocks)
    peak = peak.reshape(total_rows)
    total = total.reshape(total_rows)
    weighted = weighted.reshape(total_rows)
    highest = jnp.maximum(peak, pos)
    factor = jnp.exp(peak - highest)
    own_weight = jnp.exp(pos - highest)
    final_total = total * factor + own_weight
    final_weighted = weighted * factor + pos * own_weight
    lse = highest + jnp.log(final_total)
    loss = lse - pos
    terms = final_weighted / final_total - pos
    temp_grad = (jnp.sum(terms) / total_rows).reshape(1)
    queue_blocks = QUEUE // BLOCK
    targets = ((write_pointer[0] + block_order) % queue_blocks).astype(jnp.int32)
    new_blocks = keys.reshape(total_rows // BLOCK, BLOCK, D)
    new_queue = queue_keys.reshape(queue_blocks, BLOCK, D).at[targets].set(new_blocks).reshape(QUEUE, D)
    return loss, temp_grad, new_queue
```

```python
import functools

import jax
import jax.numpy as jnp
from jax import lax
from jax.experimental import pallas as pl
from jax.experimental.pallas import tpu as pltpu
from jax.sharding import Mesh
from jax.sharding import PartitionSpec as P

MESH = pl.DeviceIdType.MESH
ALL = ("y", "z", "c", "x")
QUEUE = ("y", "z", "c")
TOK = 128
WIDTH = 256
SLOTS = 4096
TOTAL = 16384
CHUNK = 1024
STEPS = 2 * SLOTS // CHUNK
LOG2E = 1.4426950408889634
COLORS = ((("x", "z", "y"), 0, 32), (("x", "y", "z"), 32, 32), (("z", "y", "x"), 64, 64))


def mod(value, n):
    return lax.rem(value, n)


def merge(peaks, totals, weights, c):
    peak = jnp.max(peaks, axis=0, keepdims=True)
    down = peaks - peak
    factor = jnp.exp2(down * c)
    total = jnp.sum(totals * factor, axis=0, keepdims=True)
    weight = jnp.sum((weights + down * totals) * factor, axis=0, keepdims=True)
    return peak, total, weight


def kernel(
    q_in, k_in, queue_in, log_scale, pointer, order, pos_index,
    loss_ref, grad_ref, new_ref,
    keys, qs, pool, logits, peaks, stats_out, stats_in, sums_a, sums_b, picked,
    load_sem, pair_send, pair_recv, q1_send, q1_recv, q2_send, q2_recv,
    key_send, key_recv, fwd_send, fwd_recv, st_send, st_recv, a_send, a_recv, b_send, b_recv,
):
    at = {name: lax.axis_index(name) for name in ALL}
    y, z, core, x = at["y"], at["z"], at["c"], at["x"]
    odd = mod(y + z, 2)

    def peer(**moves):
        return {name: mod(at[name] + move, 2 if name == "c" else 4) for name, move in moves.items()}

    def remote(src, dst, send, recv, device):
        return pltpu.make_async_remote_copy(
            src_ref=src, dst_ref=dst, send_sem=send, recv_sem=recv, device_id=device, device_id_type=MESH
        )

    own_q = qs.at[odd, y * (1 - odd) + z * odd, lax.div(z * (1 - odd) + y * odd, 2)]
    own_k = pool.at[y, z, core, x]
    loads = [
        pltpu.make_async_copy(q_in, own_q, load_sem.at[0]),
        pltpu.make_async_copy(k_in, own_k, load_sem.at[1]),
        pltpu.make_async_copy(queue_in, keys.at[pl.ds(0, SLOTS)], load_sem.at[2]),
    ]
    for copy in loads:
        copy.start()

    barrier = pltpu.get_barrier_semaphore()
    near = [peer(**{name: move}) for name in "xyz" for move in (1, 2, 3)] + [peer(c=1)]
    for device in near:
        pl.semaphore_signal(barrier, inc=1, device_id=device, device_id_type=MESH)
    pl.semaphore_wait(barrier, len(near))

    q1 = []
    for k in (1, 3, 2):
        q1.append(
            remote(q_in, own_q, q1_send.at[k], q1_recv.at[k], peer(y=k * odd, z=k * (1 - odd)))
        )
        q1[-1].start()
    pair = []
    for part in range(4):
        rows = pl.ds(part * 1024, 1024)
        pair.append(
            remote(
                queue_in.at[rows], keys.at[pl.ds(SLOTS + part * 1024, 1024)],
                pair_send.at[part], pair_recv.at[part], peer(c=1),
            )
        )
        pair[-1].start()

    def piece(color, free, **index):
        rings, row, count = COLORS[color]
        spot = []
        for name in "yzcx":
            if name in free:
                spot.append(slice(None))
            else:
                spot.append(index.get(name, at[name]))
        return pool.at[(*spot, pl.ds(index.get("row", row), index.get("count", count)))]

    sent = list(q1) + list(pair)

    def key_stage(color, stage):
        rings, row, count = COLORS[color]
        ring, free = rings[stage], rings[:stage]
        moves = (1, 3, 2) if stage < 2 else (1, 3)
        return [
            remote(
                k_in.at[pl.ds(row, count)] if stage == 0 else piece(color, free),
                piece(color, free),
                key_send.at[color, stage, k], key_recv.at[color, stage, k], peer(**{ring: k}),
            )
            for k in moves
        ]

    def key_last(color):
        rings, row, count = COLORS[color]
        ring, free = rings[2], rings[:2]
        half = count // 2
        copies = []
        for k, first in ((1, row), (3, row + half)):
            part = piece(color, free, **{ring: mod(at[ring] + 4 - k, 4), "row": first, "count": half})
            copies.append(
                remote(part, part, key_send.at[color, 3, k], key_recv.at[color, 3, k], peer(**{ring: k}))
            )
        return copies

    def arrivals(color, stage):
        rings, row, count = COLORS[color]
        if stage == 3:
            ring, free = rings[2], rings[:2]
            half = count // 2
            out = []
            for k, first in ((1, row), (3, row + half)):
                part = piece(color, free, **{ring: mod(at[ring] + 2, 4), "row": first, "count": half})
                out.append(remote(part, part, key_send.at[color, 3, k], key_recv.at[color, 3, k], peer(c=1)))
            return out
        ring, free = rings[stage], rings[:stage]
        moves = (1, 3, 2) if stage < 2 else (1, 3)
        out = []
        for k in moves:
            part = piece(color, free, **{ring: mod(at[ring] + 4 - k, 4)})
            out.append(remote(part, part, key_send.at[color, stage, k], key_recv.at[color, stage, k], peer(c=1)))
        return out

    def forward(color, group):
        rings, row, count = COLORS[color]
        ring, free = rings[2], rings[:2]
        move = (0, 3, 1, 2)[group]
        part = piece(color, free, **{ring: mod(at[ring] + move, 4)})
        return remote(part, part, fwd_send.at[color, group], fwd_recv.at[color, group], peer(c=1))

    def forwarded(color, group):
        rings, row, count = COLORS[color]
        ring, free = rings[2], rings[:2]
        move = (0, 3, 1, 2)[group]
        part = piece(color, free, **{ring: mod(at[ring] + move, 4), "c": 1 - core})
        return remote(part, part, fwd_send.at[color, group], fwd_recv.at[color, group], peer(c=1))

    for color in range(3):
        for copy in key_stage(color, 0):
            copy.start()
    sent += [copy for color in range(3) for copy in key_stage(color, 0)]

    scale = jnp.exp(jnp.full((1, TOK), log_scale[0], jnp.float32))
    c = scale * LOG2E
    c4 = jnp.concatenate([c] * 4, axis=1)

    lanes = lax.broadcasted_iota(jnp.int32, (1, TOK), 1)
    first_slot = ((y * 4 + z) * 2 + core) * 32
    for j in range(32):
        offset = lax.rem(first_slot + j + 1024 - pointer[0], 1024)
        picked[j] = jnp.max(jnp.where(order[...] == offset, lanes, 0))

    for copy in loads[:2]:
        copy.wait()
    scores = lax.dot_general(
        own_k[...], own_q[...], (((1,), (1,)), ((), ())), preferred_element_type=jnp.float32
    )
    rows = lax.broadcasted_iota(jnp.int32, (TOK, TOK), 0)
    positive = jnp.sum(jnp.where(rows == pos_index[...], scores, 0.0), axis=0, keepdims=True)

    def q1_spot(parity, k):
        from_y = mod(y + (4 - k) * parity, 4)
        from_z = mod(z + (4 - k) * (1 - parity), 4)
        line = from_y * (1 - parity) + from_z * parity
        return qs.at[parity, line, lax.div(from_z * (1 - parity) + from_y * parity, 2)]

    for k in (1, 2, 3):
        parity = mod(odd + k, 2)
        spot = q1_spot(parity, k)
        remote(spot, spot, q1_send.at[k], q1_recv.at[k], peer(c=1)).wait_recv()

    def q2(along, k):
        line = qs.at[0, y] if along == "y" else qs.at[1, z]
        which = 0 if along == "y" else 1
        return remote(line, line, q2_send.at[which, k], q2_recv.at[which, k], peer(**{along: k}))

    def q2_wait(k):
        for which, along in ((0, "y"), (1, "z")):
            line = qs.at[which, mod(at[along] + k, 4)]
            remote(line, line, q2_send.at[which, mod(4 - k, 4)], q2_recv.at[which, mod(4 - k, 4)], peer(c=1)).wait_recv()

    for k in (3, 1, 2):
        for along in ("y", "z"):
            q2(along, k).start()
            sent.append(q2(along, k))

    loads[2].wait()

    def tile_of(t):
        return t ^ lax.shift_right_logical(t, 1)

    def matmul(i, slot):
        t, j = lax.div(i, STEPS), lax.rem(i, STEPS)
        k = tile_of(t)
        block = keys[pl.ds(pl.multiple_of(j * CHUNK, CHUNK), CHUNK), :]
        for which, line in ((0, mod(y + k, 4)), (1, mod(z + k, 4))):
            got = lax.dot_general(
                block, qs[which, line].reshape(2 * TOK, WIDTH),
                (((1,), (1,)), ((), ())), preferred_element_type=jnp.float32,
            )
            logits[slot, :, which * 256 : which * 256 + 256] = got
            peaks[slot, :, which * 256 : which * 256 + 256] = got.reshape(CHUNK // 8, 8, 256).max(0)

    def owner(k, b):
        line_y, line_z = mod(y + k, 4), mod(z + k, 4)
        if b < 2:
            return line_y, 2 * b + mod(line_y, 2)
        return 2 * (b - 2) + mod(line_z + 1, 2), line_z

    def send_stats(t, b):
        k = tile_of(t)
        own_y, own_z = owner(k, b)
        return own_y, own_z, remote(
            stats_out.at[t, b], stats_in.at[y, z], st_send.at[t, b], st_recv.at[y, z], {"y": own_y, "z": own_z}
        )

    def events(i):
        def when(step, fn):
            pl.when(i == step)(fn)

        def pair_ready():
            for copy in pair:
                copy.wait_recv()

        def keys_two():
            for color in range(3):
                for copy in arrivals(color, 0):
                    copy.wait_recv()
                for copy in key_stage(color, 1):
                    copy.start()

        def keys_three():
            for color in range(3):
                for copy in arrivals(color, 1):
                    copy.wait_recv()
                for copy in key_stage(color, 2):
                    copy.start()
                forward(color, 0).start()

        def keys_four():
            for color in range(3):
                for copy in arrivals(color, 2):
                    copy.wait_recv()
                for copy in key_last(color):
                    copy.start()
                forward(color, 1).start()
                forward(color, 2).start()

        when(0, keys_two)
        when(2, pair_ready)
        when(STEPS - 1, lambda: q2_wait(1))
        when(9, keys_three)
        when(2 * STEPS - 1, lambda: q2_wait(3))
        when(3 * STEPS - 1, lambda: q2_wait(2))
        when(24, keys_four)

    matmul(jnp.int32(0), 0)
    steps = 4 * STEPS

    def body(i2, carry):
        for parity in range(2):
            i = i2 * 2 + parity
            t, j = lax.div(i, STEPS), lax.rem(i, STEPS)
            events(i)
            m0, l0, w0 = carry
            fresh_tile = j == 0
            m0 = jnp.where(fresh_tile, -1e30, m0)
            l0 = jnp.where(fresh_tile, 0.0, l0)
            w0 = jnp.where(fresh_tile, 0.0, w0)
            matmul(jnp.minimum(i + 1, steps - 1), 1 - parity)
            m = jnp.maximum(m0, peaks[parity])
            down = logits[parity].reshape(CHUNK // 8, 8, 512) - m[None]
            p = jnp.exp2(down * c4)
            e0 = m0 - m
            a = jnp.exp2(e0 * c4)
            l1 = l0 * a + p.sum(0)
            w1 = (w0 + e0 * l0) * a + (p * down).sum(0)
            carry = (m, l1, w1)

        @pl.when(j == STEPS - 1)
        def _():
            peak, total, weight = merge(m, l1, w1, c4)
            for b in range(4):
                cut = slice(b * TOK, (b + 1) * TOK)
                stats_out[t, b, 0:1] = peak[:, cut]
                stats_out[t, b, 1:2] = total[:, cut]
                stats_out[t, b, 2:3] = weight[:, cut]
            for b in range(4):
                own_y, own_z, copy = send_stats(t, b)
                mine = jnp.logical_and(own_y == y, own_z == z)

                @pl.when(jnp.logical_not(mine))
                def _():
                    copy.start()

                @pl.when(mine)
                def _():
                    stats_in[y, z] = stats_out[t, b]

        return carry

    zero = jnp.zeros((8, 512), jnp.float32)
    lax.fori_loop(0, steps // 2, body, (zero, zero, zero))

    for dy in range(4):
        for dz in range(4):
            if dy or dz:
                sy, sz = mod(y + dy, 4), mod(z + dz, 4)
                spot = stats_in.at[sy, sz]
                remote(spot, spot, st_send.at[0, 0], st_recv.at[sy, sz], peer(c=1)).wait_recv()
    got = stats_in[...].reshape(16, 8, TOK)
    peak = jnp.maximum(jnp.max(got[:, 0], axis=0, keepdims=True), positive)
    down = got[:, 0] - peak
    factor = jnp.exp2(down * c)
    own = positive - peak
    own_weight = jnp.exp2(own * c)
    total = jnp.sum(got[:, 1] * factor, axis=0, keepdims=True) + own_weight
    weight = (
        jnp.sum((got[:, 2] + down * got[:, 1]) * factor, axis=0, keepdims=True) + own * own_weight
    )
    loss_ref[...] = jnp.log(total) - scale * own
    terms = scale * (weight / total - own)
    mine = jnp.broadcast_to(jnp.sum(terms, axis=1, keepdims=True), (8, TOK))
    sums_a[y, z] = mine
    a_copies = []
    for dy in range(4):
        for dz in range(4):
            if dy or dz:
                copy = remote(
                    sums_a.at[y, z], sums_a.at[y, z], a_send.at[dy, dz], a_recv.at[y, z], peer(y=dy, z=dz)
                )
                copy.start()
                a_copies.append(copy)

    for color in range(3):
        for copy in arrivals(color, 3):
            copy.wait_recv()
        forward(color, 3).start()

    for dy in range(4):
        for dz in range(4):
            if dy or dz:
                sy, sz = mod(y + dy, 4), mod(z + dz, 4)
                spot = sums_a.at[sy, sz]
                remote(spot, spot, a_send.at[dy, dz], a_recv.at[sy, sz], peer(c=1)).wait_recv()
    sums_b[core, x] = jnp.sum(sums_a[...].reshape(16, 8, TOK), axis=0)
    b_copies = []
    for dc in range(2):
        for dx in range(4):
            if dc or dx:
                copy = remote(
                    sums_b.at[core, x], sums_b.at[core, x], b_send.at[dc, dx], b_recv.at[core, x], peer(c=dc, x=dx)
                )
                copy.start()
                b_copies.append(copy)

    for color in range(3):
        for group in range(4):
            forwarded(color, group).wait_recv()
    for j in range(32):
        offset = lax.rem(first_slot + j + 1024 - pointer[0], 1024)
        block = picked[j]
        hit = offset < TOK
        cut = pl.ds(j * TOK, TOK)
        new = pool[block // 32, lax.rem(block // 8, 4), lax.rem(block // 4, 2), lax.rem(block, 4)]
        new_ref[cut, :] = jnp.where(hit, new, keys[cut, :])

    for dc in range(2):
        for dx in range(4):
            if dc or dx:
                sc, sx = mod(core + dc, 2), mod(x + dx, 4)
                spot = sums_b.at[sc, sx]
                remote(spot, spot, b_send.at[dc, dx], b_recv.at[sc, sx], peer(c=1)).wait_recv()
    grand = jnp.sum(sums_b[...].reshape(8, 8, TOK), axis=0)
    grad_ref[0] = grand[0, 0] * (1.0 / TOTAL)

    for copy in sent:
        copy.wait_send()
    for color in range(3):
        for stage in (1, 2):
            for copy in key_stage(color, stage):
                copy.wait_send()
        for copy in key_last(color):
            copy.wait_send()
        for group in range(4):
            forward(color, group).wait_send()
    for t in range(4):
        for b in range(4):
            own_y, own_z, copy = send_stats(jnp.int32(t), b)

            @pl.when(jnp.logical_not(jnp.logical_and(own_y == y, own_z == z)))
            def _():
                copy.wait_send()
    for copy in a_copies + b_copies:
        copy.wait_send()


def per_device(queries, keys, queue_keys, log_scale, write_pointer, block_order, pos_index):
    vmem = pl.BlockSpec(memory_space=pltpu.VMEM)
    smem = pl.BlockSpec(memory_space=pltpu.SMEM)
    anyspace = pl.BlockSpec(memory_space=pl.ANY)
    dma = pltpu.SemaphoreType.DMA
    f32, bf16 = jnp.float32, jnp.bfloat16
    loss, grad, new = pl.pallas_call(
        kernel,
        out_shape=[
            jax.ShapeDtypeStruct((1, TOK), f32),
            jax.ShapeDtypeStruct((1,), f32),
            jax.ShapeDtypeStruct((SLOTS, WIDTH), bf16),
        ],
        in_specs=[anyspace, anyspace, anyspace, smem, smem, vmem, vmem],
        out_specs=[vmem, smem, vmem],
        scratch_shapes=[
            pltpu.VMEM((2 * SLOTS, WIDTH), bf16),
            pltpu.VMEM((2, 4, 2, TOK, WIDTH), bf16),
            pltpu.VMEM((4, 4, 2, 4, TOK, WIDTH), bf16),
            pltpu.VMEM((2, CHUNK, 512), f32),
            pltpu.VMEM((2, 8, 512), f32),
            pltpu.VMEM((4, 4, 8, TOK), f32),
            pltpu.VMEM((4, 4, 8, TOK), f32),
            pltpu.VMEM((4, 4, 8, TOK), f32),
            pltpu.VMEM((2, 4, 8, TOK), f32),
            pltpu.SMEM((32,), jnp.int32),
            dma((3,)), dma((4,)), dma((4,)), dma((4,)), dma((4,)), dma((2, 4)), dma((2, 4)),
            dma((3, 4, 4)), dma((3, 4, 4)), dma((3, 4)), dma((3, 4)), dma((4, 4)), dma((4, 4)),
            dma((4, 4)), dma((4, 4)), dma((2, 4)), dma((2, 4)),
        ],
        compiler_params=pltpu.CompilerParams(
            collective_id=0, has_side_effects=True, vmem_limit_bytes=50 << 20
        ),
    )(
        queries, keys, queue_keys, log_scale, write_pointer,
        block_order.reshape(1, TOK), pos_index.reshape(1, TOK),
    )
    return loss.reshape(TOK), grad, new


def solution(mesh):
    torus = Mesh(mesh.devices.reshape(4, 4, 2, 4), ALL)
    return jax.shard_map(
        per_device,
        mesh=torus,
        in_specs=(P(ALL, None), P(ALL, None), P(QUEUE, None), P(), P(), P(), P(ALL)),
        out_specs=(P(ALL), P(), P(QUEUE, None)),
        check_vma=False,
    )
```
